32 devices in a mesh: seq: 4 (over y, core), head: 8 (over z, x).
Axes of the slice: x: 2, y: 2, z: 4, core: 2. Of those that a mesh axis runs over, the one named last changes fastest.
Arguments:
- tokens: bfloat16 [4096, 6144], P('seq', 'head'), may hold values from -6 to 6
- proj_weight: bfloat16 [4, 6144, 1024], P(None, None, 'head'), may hold values from -0.078125 to 0.078125
- decay_rate: float32 [1024], P('head'), may hold values from 5e-05 to 0.04
- norm_gain: float32 [1024], P('head'), may hold values from 0.5 to 1.5
- pool_down: bfloat16 [16, 6144, 64], P('head'), may hold values from -0.078125 to 0.078125
- pool_up: bfloat16 [16, 64, 1024], P('head'), may hold values from -0.75 to 0.75
- span_id: int32 [4, 2], replicated, may hold values from 0 to 7, as said below
- prompt_adapter: int32 [8], replicated, may hold values from 0 to 15
- owner_pos: int32 [16], replicated, may hold values from 0 to 15, each once
- slice_len: int32 [4, 2], replicated, may hold values from 1 to 512, as said below
Outputs:
- mixed_out: bfloat16 [4096, 1024], P('seq', 'head')
- end_states: float32 [4, 2, 1024, 128], P('seq', None, 'head')
The draws below stay inside these ranges and needn't reach their ends.
Inputs may be any that keep to these rules, and one draw needn't show every extreme that they name: `span_id`: along each lane, the slices of one prompt stand on consecutive seq indices and share an id; a prompt holds 1 to 4 slices; ids of different lanes differ. `slice_len`: A slice followed in its lane by a slice of the same prompt holds 512 tokens. `owner_pos`: each pool position holds exactly one adapter.
All inputs are finite; a program needn't handle non-finite values.
Results may differ from the reference program's by a relative error of at most 0.002.
The reference program's roundings to bfloat16 on the way (of `low`) count: a program that leaves them out, or rounds other values in their place, can miss the bound.
Values may be sent and summed in bfloat16 or wider, within the bound.
A program may use at most 128 MiB of HBM per device.

```python
import math
import jax
import jax.numpy as jnp
from jax import lax

D = 6144
P_SIZE = 128
R = 64
SLICE = 512
MOST = 4
LANES = 2
HEADS = 8
ADAPTERS = 16
PROMPTS = 8
TOKENS = 4096
N_SEQ = 4


def span_layout(key):
    seg_key = jax.random.fold_in(key, 7)
    seg_sizes = jax.random.randint(seg_key, (LANES, N_SEQ), 1, MOST + 1)
    seg_sizes = seg_sizes.at[0, 0].set(min(MOST, N_SEQ))
    bounds = jnp.cumsum(seg_sizes, axis=1)
    worker_index_list = jnp.arange(N_SEQ, dtype=jnp.int32)
    tallied_total = jnp.sum((bounds[:, :, None] <= worker_index_list[None, None, :]).astype(jnp.int32), axis=1)
    lane_ids = jnp.arange(LANES, dtype=jnp.int32)
    spans = (N_SEQ * LANES - 1 - (lane_ids[:, None] * N_SEQ + tallied_total)).astype(jnp.int32)
    return spans.T


def draw_span_id(key, part):
    return span_layout(key)


def draw_slice_len(key, part):
    spans = span_layout(key)
    following = jnp.concatenate([spans[1:], jnp.full((1, LANES), -1, jnp.int32)], axis=0)
    is_last = following != spans
    ragged = jax.random.randint(jax.random.fold_in(key, 11), (N_SEQ, LANES), 1, SLICE + 1)
    return jnp.where(is_last, ragged, SLICE).astype(jnp.int32)


def draw_decay_rate(key, part):
    uniform_part = jax.random.uniform(key, (HEADS * P_SIZE,), jnp.float32)
    lower, upper = (math.log(5e-05), math.log(0.04))
    return jnp.exp(lower + uniform_part * (upper - lower)).astype(jnp.float32)


def touch_ends(array, own_key, least, high):
    longest = array.shape.index(max(array.shape))
    spots = []
    for shift in (0, 1):
        where = [jax.random.randint(jax.random.fold_in(own_key, axis), (), 0, length) for axis, length in enumerate(array.shape)]
        where[longest] = (where[longest] + shift) % array.shape[longest]
        spots.append(tuple(where))
    return array.at[spots[0]].set(least).at[spots[1]].set(high)


def levels(rng, dims, pieces, low, high):
    factor_of, own = 1.0, jax.random.fold_in(rng, 6)
    for axis_at, parts in pieces:
        steps = jnp.exp(jax.random.uniform(jax.random.fold_in(own, axis_at), (parts,), jnp.float32, low / len(pieces), high / len(pieces)))
        factor_of = factor_of * jnp.repeat(steps, dims[axis_at] // parts).reshape([-1 if axis == axis_at else 1 for axis in range(len(dims))])
    return factor_of


def noise(stream_key, extent, scale, reach, pieces=(), kind=jnp.bfloat16):
    array = scale * jax.random.normal(stream_key, extent, jnp.float32)
    if pieces:
        array = array * levels(stream_key, extent, pieces, -0.22, 0.18)
    return jnp.clip(array, -reach, reach).astype(kind)


def setup_inputs(seed: int = 0) -> dict:
    streams_of = jax.random.split(jax.random.key(seed), 11)
    tokens = noise(streams_of[0], (TOKENS, D), 1.0, 6.0, ((0, 4), (1, 8)))
    proj_weight = noise(streams_of[1], (4, D, HEADS * P_SIZE), D ** -0.5, 0.078125, ((2, 8),))
    decay_rate = draw_decay_rate(jax.random.fold_in(streams_of[10], 71), 0)
    norm_gain = jnp.clip(1.0 + 0.1 * jax.random.normal(streams_of[3], (HEADS * P_SIZE,), jnp.float32), 0.5, 1.5)
    pool_down = noise(streams_of[4], (ADAPTERS, D, R), D ** -0.5, 0.078125, ((0, 8),))
    pool_up = noise(streams_of[5], (ADAPTERS, R, HEADS * P_SIZE), R ** -0.5, 0.75, ((0, 8),))
    span_id = draw_span_id(jax.random.fold_in(streams_of[10], 71), 0)
    prompt_adapter = touch_ends(jax.random.randint(streams_of[7], (PROMPTS,), 0, ADAPTERS), jax.random.fold_in(streams_of[7], 1), 0, ADAPTERS - 1).astype(jnp.int32)
    owner_pos = jax.random.permutation(streams_of[8], ADAPTERS).astype(jnp.int32)
    slice_len = draw_slice_len(jax.random.fold_in(streams_of[10], 71), 0)
    return {"tokens": tokens, "proj_weight": proj_weight, "decay_rate": decay_rate, "norm_gain": norm_gain, "pool_down": pool_down, "pool_up": pool_up, "span_id": span_id, "prompt_adapter": prompt_adapter, "owner_pos": owner_pos, "slice_len": slice_len}


NORM_FLOOR = 1.0

def slice_layer(rows, proj_weight, down_panel, up_panel, decay_rate, norm_gain, length, start_state):
    width = proj_weight.shape[2]
    heads = width // P_SIZE
    slot_ids = jnp.arange(SLICE, dtype=jnp.int32)
    causal = slot_ids[:, None] >= slot_ids[None, :]
    query = jnp.dot(rows, proj_weight[0], preferred_element_type=jnp.float32).astype(jnp.bfloat16)
    key_unprocessed = jnp.dot(rows, proj_weight[1], preferred_element_type=jnp.float32).astype(jnp.bfloat16)
    value = jnp.dot(rows, proj_weight[2], preferred_element_type=jnp.float32).astype(jnp.bfloat16)
    lower_rank_part = jnp.dot(rows, down_panel, preferred_element_type=jnp.float32).astype(jnp.bfloat16)
    gate = jnp.dot(rows, proj_weight[3], preferred_element_type=jnp.float32) + jnp.dot(lower_rank_part, up_panel, preferred_element_type=jnp.float32)
    live = (slot_ids < length).astype(jnp.float32)
    step_log = -(live[:, None] * decay_rate[None, :] * (2.0 * jax.nn.sigmoid(gate)))
    cumul = jnp.cumsum(step_log, axis=0).reshape(SLICE, heads, P_SIZE)
    query_f = query.astype(jnp.float32).reshape(SLICE, heads, P_SIZE)
    key_f = key_unprocessed.astype(jnp.float32).reshape(SLICE, heads, P_SIZE) * (live * P_SIZE ** (-0.5))[:, None, None]
    value_f = value.astype(jnp.float32).reshape(SLICE, heads, P_SIZE)
    query_decay = query_f * jnp.exp(cumul)
    key_decay = key_f * jnp.exp(-cumul)
    attention_scores = jnp.einsum('thc,jhc->htj', query_decay, key_decay, precision=lax.Precision.HIGHEST)
    attention_scores = jnp.where(causal[None], attention_scores, 0.0)
    inner = jnp.einsum('htj,jhd->thd', attention_scores, value_f, precision=lax.Precision.HIGHEST)
    inner = inner + jnp.einsum('thc,hcd->thd', query_decay, start_state, precision=lax.Precision.HIGHEST)
    normed = inner * lax.rsqrt(jnp.maximum(lax.optimization_barrier(jnp.mean(inner * inner, axis=-1, keepdims=True)), NORM_FLOOR)) * norm_gain.reshape(heads, P_SIZE)
    out_rows = (normed * live[:, None, None]).reshape(SLICE, width).astype(jnp.bfloat16)
    last_cumul = cumul[-1]
    carried = jnp.einsum('jhc,jhd->hcd', key_f * jnp.exp(last_cumul[None] - cumul), value_f, precision=lax.Precision.HIGHEST)
    end_state = jnp.exp(last_cumul)[:, :, None] * start_state + carried
    return (out_rows, end_state)

def reference(tokens, proj_weight, decay_rate, norm_gain, pool_down, pool_up, span_id, prompt_adapter, owner_pos, slice_len):
    width = proj_weight.shape[2]
    heads = width // P_SIZE

    def device_step(preceding_value, device_index):
        out_list = []
        state_list = []
        for lane_pos in range(LANES):
            prompt = span_id[device_index, lane_pos]
            earlier = span_id[jnp.maximum(device_index - 1, 0), lane_pos]
            keep_flag = jnp.where((device_index > 0) & (prompt == earlier), 1.0, 0.0).astype(jnp.float32)
            place = owner_pos[prompt_adapter[prompt]]
            offset = ((device_index * LANES + lane_pos) * SLICE).astype(jnp.int32)
            rows = lax.dynamic_slice_in_dim(tokens, offset, SLICE, 0)
            start_state = keep_flag * preceding_value[lane_pos]
            out_rows, end_state = slice_layer(rows, proj_weight, pool_down[place], pool_up[place], decay_rate, norm_gain, slice_len[device_index, lane_pos], start_state)
            out_list.append(out_rows)
            state_list.append(end_state)
        stacked = jnp.stack(state_list)
        return (stacked, (jnp.concatenate(out_list, axis=0), stacked.reshape(LANES, width, P_SIZE)))
    initial = jnp.zeros((LANES, heads, P_SIZE, P_SIZE), jnp.float32)
    _, (outs, states) = lax.scan(device_step, initial, jnp.arange(N_SEQ, dtype=jnp.int32))
    return (outs.reshape(N_SEQ * LANES * SLICE, width), states)
```

```python
import functools
import math

import jax
import jax.numpy as jnp
from jax import lax
from jax.experimental import pallas as pl
from jax.experimental.pallas import tpu as pltpu
from jax.sharding import PartitionSpec as P

P_SIZE = 128
NORM_FLOOR = 1.0
PIECES = 4
MESH = pl.DeviceIdType.MESH
HIGHEST = lax.Precision.HIGHEST


def grid_of(n):
    across = math.isqrt(n // 2)
    if across >= 2 and 2 * across * across == n:
        return across, n // across
    return 1, n


def head_at(position, n):
    across, depth = grid_of(n)
    if across == 1:
        return position
    width = across - 1
    back = lax.div(lax.div(position, depth) + (across - 1), across)
    rest = (position - depth) * back
    row, step = lax.div(rest, width), lax.rem(rest, width)
    x = 1 + step + lax.rem(row, 2) * (width - 1 - 2 * step)
    return (1 - back) * position * across + back * ((depth - 1 - row) * across + x)


def position_of(head, n):
    across, depth = grid_of(n)
    if across == 1:
        return head
    width = across - 1
    z, x = lax.div(head, across), lax.rem(head, across)
    back = lax.div(x + across - 1, across)
    row, step = depth - 1 - z, (x - 1) * back
    moved = step + lax.rem(row, 2) * (width - 1 - 2 * step)
    return (1 - back) * z + back * (depth + row * width + moved)


def dot(a, b, precision=None):
    return jnp.dot(a, b, preferred_element_type=jnp.float32, precision=precision)


def kernel(
    n,
    n_seq,
    span_ref,
    prompt_ref,
    owner_ref,
    len_ref,
    tok_ref,
    w_hbm,
    down_hbm,
    up_ref,
    rate_ref,
    gain_ref,
    out_ref,
    state_ref,
    slots,
    wbuf,
    dbuf,
    acc,
    lacc,
    up_send,
    up_recv,
    low_send,
    low_recv,
    low_full,
    st_send,
    st_recv,
    w_sem,
    ring_send,
    ring_recv,
    up_ssem,
    up_rsem,
    rs_ssem,
    rs_rsem,
    ag_ssem,
    ag_rsem,
    st_ssem,
    st_rsem,
):
    me = lax.axis_index("head")
    seq = lax.axis_index("seq")
    rows, shard = tok_ref.shape
    lanes = span_ref.shape[1]
    per_owner = down_hbm.shape[0]
    rank = down_hbm.shape[2]
    slice_rows = rows // lanes
    piece = rows // PIECES
    half = n // 2
    here = position_of(me, n)
    right = head_at(lax.rem(here + 1, n), n)
    left = head_at(lax.rem(here + n - 1, n), n)
    toward = (right, left)

    loads = [
        pltpu.make_async_copy(w_hbm.at[c], wbuf.at[:, pl.ds(c * P_SIZE, P_SIZE)], w_sem.at[c])
        for c in range(4)
    ]
    loads.append(pltpu.make_async_copy(down_hbm, dbuf, w_sem.at[4]))

    barrier = pltpu.get_barrier_semaphore()

    def greet_head(d, carry):
        pl.semaphore_signal(
            barrier, inc=1, device_id={"head": lax.rem(me + d, n)}, device_id_type=MESH
        )
        return carry

    def greet_seq(d, carry):
        pl.semaphore_signal(
            barrier, inc=1, device_id={"seq": lax.rem(seq + d, n_seq)}, device_id_type=MESH
        )
        return carry

    lax.fori_loop(1, n, greet_head, 0)
    lax.fori_loop(1, n_seq, greet_seq, 0)
    for load in loads:
        load.start()
    pl.semaphore_wait(barrier, n - 1 + n_seq - 1)

    def hop(direction, step, p, own=False):
        span = pl.ds(p * piece, piece)
        source = tok_ref.at[span] if own else slots.at[direction, step - 2, span]
        return pltpu.make_async_remote_copy(
            src_ref=source,
            dst_ref=slots.at[direction, step - 1, span],
            send_sem=ring_send.at[direction, step - 1, p],
            recv_sem=ring_recv.at[direction, step - 1, p],
            device_id={"head": toward[direction]},
            device_id_type=MESH,
        )

    def long_way(direction, p):
        return p % 2 == direction

    for k in range(PIECES):
        for direction in range(2):
            hop(direction, 1, (k + direction) % PIECES, own=True).start()

    places = [owner_ref[prompt_ref[span_ref[seq, j]]] for j in range(lanes)]
    owned = [
        [jnp.where(places[j] == me * per_owner + s, 1.0, 0.0).astype(jnp.float32) for s in range(per_owner)]
        for j in range(lanes)
    ]

    for j in range(lanes):
        mine = sum(owned[j][s] * up_ref[s].astype(jnp.float32) for s in range(per_owner)).astype(jnp.bfloat16)
        for i in range(n):
            up_send[i, pl.ds(j * rank, rank), :] = mine[:, i * P_SIZE : (i + 1) * P_SIZE]

    def up_copy(d):
        peer = lax.rem(me + d, n)
        return pltpu.make_async_remote_copy(
            src_ref=up_send.at[peer],
            dst_ref=up_recv.at[d],
            send_sem=up_ssem.at[d],
            recv_sem=up_rsem.at[d],
            device_id={"head": peer},
            device_id_type=MESH,
        )

    def up_start(d, carry):
        up_copy(d).start()
        return carry

    lax.fori_loop(1, n, up_start, 0)
    up_recv[0] = up_send[me]

    for load in loads:
        load.wait()

    def multiply(x, span, origin, first=False):
        deep = pl.ds(pl.multiple_of(origin * shard, 64), shard)
        gained = dot(x, wbuf[deep, :])
        lows = [dot(x, dbuf[s, deep, :]) for s in range(per_owner)]
        if first:
            acc[span, :] = gained
            for s in range(per_owner):
                lacc[s, span, :] = lows[s]
        else:
            acc[span, :] += gained
            for s in range(per_owner):
                lacc[s, span, :] += lows[s]

    def own_piece(p, carry):
        span = pl.ds(pl.multiple_of(p * piece, piece), piece)
        multiply(tok_ref[span, :], span, me, first=True)
        return carry

    lax.fori_loop(0, PIECES, own_piece, 0)

    def arrive(step, forward, present):
        order = [((k + d) % PIECES, d) for k in range(PIECES) for d in range(2)]
        order = [(p, d) for p, d in order if present(d, p)]
        for p, d in order:
            hop(d, step, p).wait_recv() if not isinstance(step, int) or step > 1 else hop(d, 1, p, own=True).wait_recv()
            if forward(d, p):
                hop(d, step + 1, p).start()
            sign = n - step if d == 0 else step
            origin = head_at(lax.rem(here + sign, n), n)
            span = pl.ds(p * piece, piece)
            multiply(slots[d, step - 1, span, :], span, origin)

    everything = lambda d, p: True
    nothing = lambda d, p: False
    if half >= 2:
        arrive(1, everything if half > 2 else long_way, everything)
    if half > 3:

        def middle(step, carry):
            arrive(step, everything, everything)
            return carry

        lax.fori_loop(2, half - 1, middle, 0)
    if half > 2:
        arrive(half - 1, long_way, everything)
    arrive(half, nothing, long_way)

    width = lanes * rank
    for j in range(lanes):
        span = pl.ds(j * slice_rows, slice_rows)
        mine = sum(owned[j][s] * lacc[s, span, :] for s in range(per_owner)).astype(jnp.bfloat16)
        low_send[:, pl.ds(j * rank, rank)] = mine
    block = slice_rows // n

    def rs_copy(d):
        peer = lax.rem(me + d, n)
        return pltpu.make_async_remote_copy(
            src_ref=low_send.at[pl.ds(pl.multiple_of(peer * block, block), block)],
            dst_ref=low_recv.at[d],
            send_sem=rs_ssem.at[d],
            recv_sem=rs_rsem.at[d],
            device_id={"head": peer},
            device_id_type=MESH,
        )

    def ag_copy(d):
        peer = lax.rem(me + d, n)
        return pltpu.make_async_remote_copy(
            src_ref=low_recv.at[0],
            dst_ref=low_full.at[me],
            send_sem=ag_ssem.at[d],
            recv_sem=ag_rsem.at[d],
            device_id={"head": peer},
            device_id_type=MESH,
        )

    def ag_arrival(d):
        peer = lax.rem(me + n - d, n)
        return pltpu.make_async_remote_copy(
            src_ref=low_recv.at[0],
            dst_ref=low_full.at[peer],
            send_sem=ag_ssem.at[d],
            recv_sem=ag_rsem.at[d],
            device_id={"head": peer},
            device_id_type=MESH,
        )

    def each(count, act):
        def turn(d, carry):
            act(d)
            return carry

        lax.fori_loop(1, count, turn, 0)

    each(n, lambda d: rs_copy(d).start())
    each(n, lambda d: up_copy(d).wait_recv())
    up = jnp.sum(up_recv[...].astype(jnp.float32), axis=0).astype(jnp.bfloat16)
    total = low_send[pl.ds(pl.multiple_of(me * block, block), block), :].astype(jnp.float32)
    each(n, lambda d: rs_copy(d).wait_recv())
    for d in range(1, n):
        total = total + low_recv[d].astype(jnp.float32)
    low_recv[0] = total.astype(jnp.bfloat16)
    each(n, lambda d: ag_copy(d).start())
    low_full[me] = total.astype(jnp.bfloat16)

    slot_ids = lax.broadcasted_iota(jnp.int32, (slice_rows, 1), 0)
    causal = lax.broadcasted_iota(jnp.int32, (slice_rows, slice_rows), 0) >= lax.broadcasted_iota(
        jnp.int32, (slice_rows, slice_rows), 1
    )
    triangle = jnp.where(causal, 1.0, 0.0).astype(jnp.float32)
    columns = lax.broadcasted_iota(jnp.int32, (1, width), 1)
    each(n, lambda d: ag_arrival(d).wait_recv())
    low = low_full[...].reshape(slice_rows, width).astype(jnp.float32)

    kept = []
    for j in range(lanes):
        span = pl.ds(j * slice_rows, slice_rows)
        own = (columns >= j * rank) & (columns < (j + 1) * rank)
        gate = acc[span, pl.ds(3 * P_SIZE, P_SIZE)] + dot(jnp.where(own, low, 0.0).astype(jnp.bfloat16), up)
        live = jnp.where(slot_ids < len_ref[seq, j], 1.0, 0.0).astype(jnp.float32)
        step_log = -(live * rate_ref[...] * (2.0 * jax.nn.sigmoid(gate)))
        cumul = dot(triangle, step_log, HIGHEST)
        query = acc[span, pl.ds(0, P_SIZE)].astype(jnp.bfloat16).astype(jnp.float32)
        key = acc[span, pl.ds(P_SIZE, P_SIZE)].astype(jnp.bfloat16).astype(jnp.float32) * (
            live * P_SIZE ** (-0.5)
        )
        value = acc[span, pl.ds(2 * P_SIZE, P_SIZE)].astype(jnp.bfloat16).astype(jnp.float32)
        last = cumul[slice_rows - 1 :, :]
        carried = lax.dot_general(
            key * jnp.exp(last - cumul),
            value,
            (((0,), (0,)), ((), ())),
            precision=HIGHEST,
            preferred_element_type=jnp.float32,
        )
        st_send[j, pl.ds(0, P_SIZE), :] = carried
        st_send[j, pl.ds(P_SIZE, 8), :] = jnp.broadcast_to(jnp.exp(last), (8, P_SIZE))
        kept.append((live, query * jnp.exp(cumul), key * jnp.exp(-cumul), value))

    def st_copy(d):
        return pltpu.make_async_remote_copy(
            src_ref=st_send,
            dst_ref=st_recv.at[seq],
            send_sem=st_ssem.at[d],
            recv_sem=st_rsem.at[d],
            device_id={"seq": lax.rem(seq + d, n_seq)},
            device_id_type=MESH,
        )

    def st_arrival(d):
        peer = lax.rem(seq + n_seq - d, n_seq)
        return pltpu.make_async_remote_copy(
            src_ref=st_send,
            dst_ref=st_recv.at[peer],
            send_sem=st_ssem.at[d],
            recv_sem=st_rsem.at[d],
            device_id={"seq": peer},
            device_id_type=MESH,
        )

    each(n_seq, lambda d: st_copy(d).start())
    st_recv[seq] = st_send[...]

    inners = []
    for j in range(lanes):
        live, query_decay, key_decay, value = kept[j]
        scores = lax.dot_general(
            query_decay,
            key_decay,
            (((1,), (1,)), ((), ())),
            precision=HIGHEST,
            preferred_element_type=jnp.float32,
        )
        inners.append(dot(jnp.where(causal, scores, 0.0), value, HIGHEST))

    each(n_seq, lambda d: st_arrival(d).wait_recv())
    for j in range(lanes):
        live, query_decay, _, _ = kept[j]
        span = pl.ds(j * slice_rows, slice_rows)
        ended = jnp.zeros((P_SIZE, P_SIZE), jnp.float32)
        start = ended
        final = ended
        for k in range(n_seq):
            if k:
                same = jnp.where(span_ref[k, j] == span_ref[k - 1, j], 1.0, 0.0).astype(jnp.float32)
                begun = same * ended
            else:
                begun = ended
            decay = jnp.broadcast_to(st_recv[k, j, pl.ds(P_SIZE, 1), :], (P_SIZE, P_SIZE)).T
            ended = decay * begun + st_recv[k, j, pl.ds(0, P_SIZE), :]
            at = jnp.where(seq == k, 1.0, 0.0).astype(jnp.float32)
            start = start + at * begun
            final = final + at * ended
        inner = inners[j] + dot(query_decay, start, HIGHEST)
        scale = lax.rsqrt(jnp.maximum(jnp.mean(inner * inner, axis=-1, keepdims=True), NORM_FLOOR))
        out_ref[span, :] = (inner * scale * gain_ref[...] * live).astype(jnp.bfloat16)
        state_ref[0, j] = final

    each(n, lambda d: up_copy(d).wait_send())
    each(n, lambda d: rs_copy(d).wait_send())
    each(n, lambda d: ag_copy(d).wait_send())
    each(n_seq, lambda d: st_copy(d).wait_send())
    for p in range(PIECES):
        for direction in range(2):
            hop(direction, 1, p, own=True).wait_send()
    for direction in range(2):
        for p in range(PIECES):
            reach = half if long_way(direction, p) else half - 1

            def drained(step, carry):
                hop(direction, step, p).wait_send()
                return carry

            lax.fori_loop(2, reach + 1, drained, 0)


def solution(mesh):
    n, n_seq = mesh.shape["head"], mesh.shape["seq"]

    def body(
        tokens,
        proj_weight,
        decay_rate,
        norm_gain,
        pool_down,
        pool_up,
        span_id,
        prompt_adapter,
        owner_pos,
        slice_len,
    ):
        rows, shard = tokens.shape
        model = proj_weight.shape[1]
        lanes = span_id.shape[1]
        per_owner, _, rank = pool_down.shape
        slice_rows = rows // lanes
        width = lanes * rank
        smem = pl.BlockSpec(memory_space=pltpu.SMEM)
        vmem = pl.BlockSpec(memory_space=pltpu.VMEM)
        hbm = pl.BlockSpec(memory_space=pl.ANY)
        dma = pltpu.SemaphoreType.DMA
        return pl.pallas_call(
            functools.partial(kernel, n, n_seq),
            out_shape=(
                jax.ShapeDtypeStruct((rows, P_SIZE), jnp.bfloat16),
                jax.ShapeDtypeStruct((1, lanes, P_SIZE, P_SIZE), jnp.float32),
            ),
            in_specs=[smem, smem, smem, smem, vmem, hbm, hbm, vmem, vmem, vmem],
            out_specs=(vmem, vmem),
            scratch_shapes=[
                pltpu.VMEM((2, n // 2, rows, shard), jnp.bfloat16),
                pltpu.VMEM((model, 4 * P_SIZE), jnp.bfloat16),
                pltpu.VMEM((per_owner, model, rank), jnp.bfloat16),
                pltpu.VMEM((rows, 4 * P_SIZE), jnp.float32),
                pltpu.VMEM((per_owner, rows, rank), jnp.float32),
                pltpu.VMEM((n, width, P_SIZE), jnp.bfloat16),
                pltpu.VMEM((n, width, P_SIZE), jnp.bfloat16),
                pltpu.VMEM((slice_rows, width), jnp.bfloat16),
                pltpu.VMEM((n, slice_rows // n, width), jnp.bfloat16),
                pltpu.VMEM((n, slice_rows // n, width), jnp.bfloat16),
                pltpu.VMEM((lanes, P_SIZE + 8, P_SIZE), jnp.float32),
                pltpu.VMEM((n_seq, lanes, P_SIZE + 8, P_SIZE), jnp.float32),
                dma((5,)),
                dma((2, n // 2, PIECES)),
                dma((2, n // 2, PIECES)),
                dma((n,)),
                dma((n,)),
                dma((n,)),
                dma((n,)),
                dma((n,)),
                dma((n,)),
                dma((n_seq,)),
                dma((n_seq,)),
            ],
            compiler_params=pltpu.CompilerParams(
                collective_id=0, has_side_effects=True, vmem_limit_bytes=58 * 1024 * 1024
            ),
        )(
            span_id,
            prompt_adapter,
            owner_pos,
            slice_len,
            tokens,
            proj_weight,
            pool_down,
            pool_up,
            decay_rate.reshape(1, -1),
            norm_gain.reshape(1, -1),
        )

    in_specs = (
        P("seq", "head"),
        P(None, None, "head"),
        P("head"),
        P("head"),
        P("head", None, None),
        P("head", None, None),
        P(),
        P(),
        P(),
        P(),
    )
    out_specs = (P("seq", "head"), P("seq", None, "head", None))
    return jax.shard_map(body, mesh=mesh, in_specs=in_specs, out_specs=out_specs, check_vma=False)
```

```python
import functools
import math

import jax
import jax.numpy as jnp
from jax import lax
from jax.experimental import pallas as pl
from jax.experimental.pallas import tpu as pltpu
from jax.sharding import PartitionSpec as P

P_SIZE = 128
NORM_FLOOR = 1.0
PIECES = 2
MESH = pl.DeviceIdType.MESH
HIGHEST = lax.Precision.HIGHEST


def grid_of(n):
    across = math.isqrt(n // 2)
    if across >= 2 and 2 * across * across == n:
        return across, n // across
    return 1, n


def head_at(position, n):
    across, depth = grid_of(n)
    if across == 1:
        return position
    width = across - 1
    back = lax.div(lax.div(position, depth) + (across - 1), across)
    rest = (position - depth) * back
    row, step = lax.div(rest, width), lax.rem(rest, width)
    x = 1 + step + lax.rem(row, 2) * (width - 1 - 2 * step)
    return (1 - back) * position * across + back * ((depth - 1 - row) * across + x)


def position_of(head, n):
    across, depth = grid_of(n)
    if across == 1:
        return head
    width = across - 1
    z, x = lax.div(head, across), lax.rem(head, across)
    back = lax.div(x + across - 1, across)
    row, step = depth - 1 - z, (x - 1) * back
    moved = step + lax.rem(row, 2) * (width - 1 - 2 * step)
    return (1 - back) * z + back * (depth + row * width + moved)


def dot(a, b, precision=None):
    return jnp.dot(a, b, preferred_element_type=jnp.float32, precision=precision)


def kernel(
    n,
    n_seq,
    span_ref,
    prompt_ref,
    owner_ref,
    len_ref,
    tok_ref,
    w_hbm,
    down_hbm,
    up_ref,
    rate_ref,
    gain_ref,
    out_ref,
    state_ref,
    slots,
    wbuf,
    dbuf,
    acc,
    up_send,
    up_recv,
    low_send,
    low_recv,
    low_full,
    st_send,
    st_recv,
    w_sem,
    ring_send,
    ring_recv,
    up_ssem,
    up_rsem,
    rs_ssem,
    rs_rsem,
    ag_ssem,
    ag_rsem,
    st_ssem,
    st_rsem,
):
    me = lax.axis_index("head")
    seq = lax.axis_index("seq")
    rows, shard = tok_ref.shape
    lanes = span_ref.shape[0]
    per_owner = down_hbm.shape[0]
    rank = down_hbm.shape[1]
    slice_rows = rows // lanes
    piece = slice_rows // PIECES
    pieces = lanes * PIECES
    half = n // 2
    here = position_of(me, n)
    right = head_at(lax.rem(here + 1, n), n)
    left = head_at(lax.rem(here + n - 1, n), n)
    toward = (right, left)

    loads = [
        pltpu.make_async_copy(w_hbm.at[c], wbuf.at[:, pl.ds(c * P_SIZE, P_SIZE)], w_sem.at[c])
        for c in range(4)
    ]
    loads += [
        pltpu.make_async_copy(down_hbm.at[s], dbuf.at[pl.ds(s * rank, rank)], w_sem.at[4 + s])
        for s in range(per_owner)
    ]

    barrier = pltpu.get_barrier_semaphore()

    def greet_head(d, carry):
        pl.semaphore_signal(
            barrier, inc=1, device_id={"head": lax.rem(me + d, n)}, device_id_type=MESH
        )
        return carry

    def greet_seq(d, carry):
        pl.semaphore_signal(
            barrier, inc=1, device_id={"seq": lax.rem(seq + d, n_seq)}, device_id_type=MESH
        )
        return carry

    lax.fori_loop(1, n, greet_head, 0)
    lax.fori_loop(1, n_seq, greet_seq, 0)
    for load in loads:
        load.start()
    pl.semaphore_wait(barrier, n - 1 + n_seq - 1)

    def hop(direction, step, p, own=False):
        span = pl.ds(p * piece, piece)
        source = tok_ref.at[span] if own else slots.at[direction, step - 2, span]
        return pltpu.make_async_remote_copy(
            src_ref=source,
            dst_ref=slots.at[direction, step - 1, span],
            send_sem=ring_send.at[direction, step - 1, p],
            recv_sem=ring_recv.at[direction, step - 1, p],
            device_id={"head": toward[direction]},
            device_id_type=MESH,
        )

    def long_way(direction, p):
        return p % 2 == direction

    def depart(lane):
        for k in range(PIECES):
            for direction in range(2):
                hop(direction, 1, lane * PIECES + (k + direction) % PIECES, own=True).start()

    depart(0)

    places = [owner_ref[prompt_ref[span_ref[j, seq]]] for j in range(lanes)]
    owned = [
        [jnp.where(places[j] == me * per_owner + s, 1.0, 0.0).astype(jnp.float32) for s in range(per_owner)]
        for j in range(lanes)
    ]

    for j in range(lanes):
        mine = sum(owned[j][s] * up_ref[s].astype(jnp.float32) for s in range(per_owner)).astype(jnp.bfloat16)
        for i in range(n):
            up_send[i, pl.ds(j * rank, rank), :] = mine[:, i * P_SIZE : (i + 1) * P_SIZE]

    def up_copy(d):
        peer = lax.rem(me + d, n)
        return pltpu.make_async_remote_copy(
            src_ref=up_send.at[peer],
            dst_ref=up_recv.at[d],
            send_sem=up_ssem.at[d],
            recv_sem=up_rsem.at[d],
            device_id={"head": peer},
            device_id_type=MESH,
        )

    def up_start(d, carry):
        up_copy(d).start()
        return carry

    lax.fori_loop(1, n, up_start, 0)
    up_recv[0] = up_send[me]

    for load in loads:
        load.wait()

    model = wbuf.shape[0]
    strip = model // 12

    def turn_strip(i, carry):
        deep = pl.ds(pl.multiple_of(i * strip, strip), strip)
        wbuf[deep, pl.ds(4 * P_SIZE, per_owner * rank)] = dbuf[:, deep].T
        return carry

    lax.fori_loop(0, 12, turn_strip, 0)

    def multiply(x, span, origin, first=False):
        deep = pl.ds(pl.multiple_of(origin * shard, 64), shard)
        gained = dot(x, wbuf[deep, :])
        if first:
            acc[span, :] = gained
        else:
            acc[span, :] += gained

    def own_piece(p, carry):
        span = pl.ds(pl.multiple_of(p * piece, piece), piece)
        multiply(tok_ref[span, :], span, me, first=True)
        return carry

    lax.fori_loop(0, pieces, own_piece, 0)

    def arrive(lane, step, forward, present):
        order = [(lane * PIECES + (k + d) % PIECES, d) for k in range(PIECES) for d in range(2)]
        for p, d in order:
            if not present(d, p):
                continue
            own = isinstance(step, int) and step == 1
            hop(d, step, p, own=own).wait_recv()
            if forward(d, p):
                hop(d, step + 1, p).start()
            sign = n - step if d == 0 else step
            origin = head_at(lax.rem(here + sign, n), n)
            span = pl.ds(p * piece, piece)
            multiply(slots[d, step - 1, span, :], span, origin)

    everything = lambda d, p: True
    nothing = lambda d, p: False

    def forwards(step):
        return everything if step < half - 1 else long_way if step == half - 1 else nothing

    def each(count, act):
        def turn(d, carry):
            act(d)
            return carry

        lax.fori_loop(1, count, turn, 0)

    block = slice_rows // n

    def rs_copy(j, d):
        peer = lax.rem(me + d, n)
        return pltpu.make_async_remote_copy(
            src_ref=low_send.at[j, pl.ds(pl.multiple_of(peer * block, block), block)],
            dst_ref=low_recv.at[j, d],
            send_sem=rs_ssem.at[j, d],
            recv_sem=rs_rsem.at[j, d],
            device_id={"head": peer},
            device_id_type=MESH,
        )

    def ag_copy(j, d):
        peer = lax.rem(me + d, n)
        return pltpu.make_async_remote_copy(
            src_ref=low_recv.at[j, 0],
            dst_ref=low_full.at[j, me],
            send_sem=ag_ssem.at[j, d],
            recv_sem=ag_rsem.at[j, d],
            device_id={"head": peer},
            device_id_type=MESH,
        )

    def ag_arrival(j, d):
        peer = lax.rem(me + n - d, n)
        return pltpu.make_async_remote_copy(
            src_ref=low_recv.at[j, 0],
            dst_ref=low_full.at[j, peer],
            send_sem=ag_ssem.at[j, d],
            recv_sem=ag_rsem.at[j, d],
            device_id={"head": peer},
            device_id_type=MESH,
        )

    def st_copy(j, d):
        return pltpu.make_async_remote_copy(
            src_ref=st_send.at[j],
            dst_ref=st_recv.at[j, seq],
            send_sem=st_ssem.at[j, d],
            recv_sem=st_rsem.at[j, d],
            device_id={"seq": lax.rem(seq + d, n_seq)},
            device_id_type=MESH,
        )

    def st_arrival(j, d):
        peer = lax.rem(seq + n_seq - d, n_seq)
        return pltpu.make_async_remote_copy(
            src_ref=st_send.at[j],
            dst_ref=st_recv.at[j, peer],
            send_sem=st_ssem.at[j, d],
            recv_sem=st_rsem.at[j, d],
            device_id={"seq": peer},
            device_id_type=MESH,
        )

    slot_ids = lax.broadcasted_iota(jnp.int32, (slice_rows, 1), 0)

    def causal():
        shape = (slice_rows, slice_rows)
        return lax.broadcasted_iota(jnp.int32, shape, 0) >= lax.broadcasted_iota(jnp.int32, shape, 1)

    def alive(j):
        return jnp.where(slot_ids < len_ref[j, seq], 1.0, 0.0).astype(jnp.float32)

    def low_scatter(j):
        span = pl.ds(j * slice_rows, slice_rows)
        lows = acc[span, pl.ds(4 * P_SIZE, per_owner * rank)]
        mine = sum(owned[j][s] * lows[:, s * rank : (s + 1) * rank] for s in range(per_owner))
        low_send[j] = mine.astype(jnp.bfloat16)
        each(n, lambda d: rs_copy(j, d).start())

    def low_gather(j):
        each(n, lambda d: rs_copy(j, d).wait_recv())
        total = low_send[j, pl.ds(pl.multiple_of(me * block, block), block), :].astype(jnp.float32)
        for d in range(1, n):
            total = total + low_recv[j, d].astype(jnp.float32)
        low_recv[j, 0] = total.astype(jnp.bfloat16)
        each(n, lambda d: ag_copy(j, d).start())
        low_full[j, me] = total.astype(jnp.bfloat16)

    def gates(j):
        span = pl.ds(j * slice_rows, slice_rows)
        up = jnp.sum(up_recv[:, pl.ds(j * rank, rank), :].astype(jnp.float32), axis=0).astype(jnp.bfloat16)
        each(n, lambda d: ag_arrival(j, d).wait_recv())
        gate = acc[span, pl.ds(3 * P_SIZE, P_SIZE)] + dot(low_full[j].reshape(slice_rows, rank), up)
        live = alive(j)
        step_log = -(live * rate_ref[...] * (2.0 * jax.nn.sigmoid(gate)))
        triangle = jnp.where(causal(), 1.0, 0.0).astype(jnp.float32)
        cumul = dot(triangle, step_log, HIGHEST)
        query = acc[span, pl.ds(0, P_SIZE)].astype(jnp.bfloat16).astype(jnp.float32)
        key = acc[span, pl.ds(P_SIZE, P_SIZE)].astype(jnp.bfloat16).astype(jnp.float32) * (
            live * P_SIZE ** (-0.5)
        )
        value = acc[span, pl.ds(2 * P_SIZE, P_SIZE)].astype(jnp.bfloat16).astype(jnp.float32)
        last = cumul[slice_rows - 1 :, :]
        carried = lax.dot_general(
            key * jnp.exp(last - cumul),
            value,
            (((0,), (0,)), ((), ())),
            precision=HIGHEST,
            preferred_element_type=jnp.float32,
        )
        st_send[j, pl.ds(0, P_SIZE), :] = carried
        st_send[j, pl.ds(P_SIZE, 8), :] = jnp.broadcast_to(jnp.exp(last), (8, P_SIZE))
        each(n_seq, lambda d: st_copy(j, d).start())
        st_recv[j, seq] = st_send[j]
        acc[span, pl.ds(0, P_SIZE)] = query * jnp.exp(cumul)
        acc[span, pl.ds(P_SIZE, P_SIZE)] = key * jnp.exp(-cumul)
        acc[span, pl.ds(2 * P_SIZE, P_SIZE)] = value

    def attend(j):
        span = pl.ds(j * slice_rows, slice_rows)
        scores = lax.dot_general(
            acc[span, pl.ds(0, P_SIZE)],
            acc[span, pl.ds(P_SIZE, P_SIZE)],
            (((1,), (1,)), ((), ())),
            precision=HIGHEST,
            preferred_element_type=jnp.float32,
        )
        acc[span, pl.ds(3 * P_SIZE, P_SIZE)] = dot(
            jnp.where(causal(), scores, 0.0), acc[span, pl.ds(2 * P_SIZE, P_SIZE)], HIGHEST
        )

    def finish(j):
        span = pl.ds(j * slice_rows, slice_rows)
        each(n_seq, lambda d: st_arrival(j, d).wait_recv())
        ended = jnp.zeros((P_SIZE, P_SIZE), jnp.float32)
        start = ended
        final = ended
        for k in range(n_seq):
            if k:
                same = jnp.where(span_ref[j, k] == span_ref[j, k - 1], 1.0, 0.0).astype(jnp.float32)
                begun = same * ended
            else:
                begun = ended
            decay = jnp.broadcast_to(st_recv[j, k, pl.ds(P_SIZE, 1), :], (P_SIZE, P_SIZE)).T
            ended = decay * begun + st_recv[j, k, pl.ds(0, P_SIZE), :]
            at = jnp.where(seq == k, 1.0, 0.0).astype(jnp.float32)
            start = start + at * begun
            final = final + at * ended
        inner = acc[span, pl.ds(3 * P_SIZE, P_SIZE)] + dot(acc[span, pl.ds(0, P_SIZE)], start, HIGHEST)
        scale = lax.rsqrt(jnp.maximum(jnp.mean(inner * inner, axis=-1, keepdims=True), NORM_FLOOR))
        out_ref[span, :] = (inner * scale * gain_ref[...] * alive(j)).astype(jnp.bfloat16)
        state_ref[0, j] = final

    stages = (low_scatter, low_gather, gates, attend, finish)
    todo = []
    for j in range(lanes):
        for step in range(1, half + 1):
            if step == half and j + 1 < lanes:
                depart(j + 1)
            arrive(j, step, forwards(step), everything if step < half else long_way)
            if j == 0 and step == half:
                each(n, lambda d: up_copy(d).wait_recv())
            if todo:
                todo.pop(0)()
        while todo:
            todo.pop(0)()
        todo = [functools.partial(stage, j) for stage in stages]
        todo.pop(0)()
    while todo:
        todo.pop(0)()

    each(n, lambda d: up_copy(d).wait_send())
    for j in range(lanes):
        each(n, lambda d: rs_copy(j, d).wait_send())
        each(n, lambda d: ag_copy(j, d).wait_send())
        each(n_seq, lambda d: st_copy(j, d).wait_send())
    for p in range(pieces):
        for direction in range(2):
            hop(direction, 1, p, own=True).wait_send()
    for direction in range(2):
        for p in range(pieces):
            reach = half if long_way(direction, p) else half - 1

            def drained(step, carry):
                hop(direction, step, p).wait_send()
                return carry

            lax.fori_loop(2, reach + 1, drained, 0)


def solution(mesh):
    n, n_seq = mesh.shape["head"], mesh.shape["seq"]

    def body(
        tokens,
        proj_weight,
        decay_rate,
        norm_gain,
        pool_down,
        pool_up,
        span_id,
        prompt_adapter,
        owner_pos,
        slice_len,
    ):
        rows, shard = tokens.shape
        model = proj_weight.shape[1]
        lanes = span_id.shape[1]
        per_owner, _, rank = pool_down.shape
        slice_rows = rows // lanes
        width = lanes * rank
        smem = pl.BlockSpec(memory_space=pltpu.SMEM)
        vmem = pl.BlockSpec(memory_space=pltpu.VMEM)
        hbm = pl.BlockSpec(memory_space=pl.ANY)
        dma = pltpu.SemaphoreType.DMA
        return pl.pallas_call(
            functools.partial(kernel, n, n_seq),
            out_shape=(
                jax.ShapeDtypeStruct((rows, P_SIZE), jnp.bfloat16),
                jax.ShapeDtypeStruct((1, lanes, P_SIZE, P_SIZE), jnp.float32),
            ),
            in_specs=[smem, smem, smem, smem, vmem, hbm, hbm, vmem, vmem, vmem],
            out_specs=(vmem, vmem),
            scratch_shapes=[
                pltpu.VMEM((2, n // 2, rows, shard), jnp.bfloat16),
                pltpu.VMEM((model, 4 * P_SIZE + per_owner * rank), jnp.bfloat16),
                pltpu.VMEM((per_owner * rank, model), jnp.bfloat16),
                pltpu.VMEM((rows, 4 * P_SIZE + per_owner * rank), jnp.float32),
                pltpu.VMEM((n, width, P_SIZE), jnp.bfloat16),
                pltpu.VMEM((n, width, P_SIZE), jnp.bfloat16),
                pltpu.VMEM((lanes, slice_rows, rank), jnp.bfloat16),
                pltpu.VMEM((lanes, n, slice_rows // n, rank), jnp.bfloat16),
                pltpu.VMEM((lanes, n, slice_rows // n, rank), jnp.bfloat16),
                pltpu.VMEM((lanes, P_SIZE + 8, P_SIZE), jnp.float32),
                pltpu.VMEM((lanes, n_seq, P_SIZE + 8, P_SIZE), jnp.float32),
                dma((4 + per_owner,)),
                dma((2, n // 2, lanes * PIECES)),
                dma((2, n // 2, lanes * PIECES)),
                dma((n,)),
                dma((n,)),
                dma((lanes, n)),
                dma((lanes, n)),
                dma((lanes, n)),
                dma((lanes, n)),
                dma((lanes, n_seq)),
                dma((lanes, n_seq)),
            ],
            compiler_params=pltpu.CompilerParams(
                collective_id=0, has_side_effects=True, vmem_limit_bytes=58 * 1024 * 1024
            ),
        )(
            span_id.T,
            prompt_adapter,
            owner_pos,
            slice_len.T,
            tokens,
            proj_weight,
            jnp.swapaxes(pool_down, 1, 2),
            pool_up,
            decay_rate.reshape(1, -1),
            norm_gain.reshape(1, -1),
        )

    in_specs = (
        P("seq", "head"),
        P(None, None, "head"),
        P("head"),
        P("head"),
        P("head", None, None),
        P("head", None, None),
        P(),
        P(),
        P(),
        P(),
    )
    out_specs = (P("seq", "head"), P("seq", None, "head", None))
    return jax.shard_map(body, mesh=mesh, in_specs=in_specs, out_specs=out_specs, check_vma=False)
```

```python
import functools
import math

import jax
import jax.numpy as jnp
from jax import lax
from jax.experimental import pallas as pl
from jax.experimental.pallas import tpu as pltpu
from jax.sharding import PartitionSpec as P

P_SIZE = 128
NORM_FLOOR = 1.0
PIECES = 4
MESH = pl.DeviceIdType.MESH
HIGHEST = lax.Precision.HIGHEST


def grid_of(n):
    across = math.isqrt(n // 2)
    if across >= 2 and 2 * across * across == n:
        return across, n // across
    return 1, n


def head_at(position, n):
    across, depth = grid_of(n)
    if across == 1:
        return position
    width = across - 1
    back = lax.div(lax.div(position, depth) + (across - 1), across)
    rest = (position - depth) * back
    row, step = lax.div(rest, width), lax.rem(rest, width)
    x = 1 + step + lax.rem(row, 2) * (width - 1 - 2 * step)
    return (1 - back) * position * across + back * ((depth - 1 - row) * across + x)


def position_of(head, n):
    across, depth = grid_of(n)
    if across == 1:
        return head
    width = across - 1
    z, x = lax.div(head, across), lax.rem(head, across)
    back = lax.div(x + across - 1, across)
    row, step = depth - 1 - z, (x - 1) * back
    moved = step + lax.rem(row, 2) * (width - 1 - 2 * step)
    return (1 - back) * z + back * (depth + row * width + moved)


def dot(a, b, precision=None):
    return jnp.dot(a, b, preferred_element_type=jnp.float32, precision=precision)


def kernel(
    n,
    n_seq,
    span_ref,
    prompt_ref,
    owner_ref,
    len_ref,
    tok_ref,
    w_hbm,
    down_hbm,
    up_ref,
    rate_ref,
    gain_ref,
    out_ref,
    state_ref,
    slots,
    wbuf,
    dbuf,
    dturn,
    acc,
    lacc,
    up_send,
    up_recv,
    low_send,
    low_recv,
    low_full,
    st_send,
    st_recv,
    w_sem,
    ring_send,
    ring_recv,
    up_ssem,
    up_rsem,
    rs_ssem,
    rs_rsem,
    ag_ssem,
    ag_rsem,
    st_ssem,
    st_rsem,
):
    me = lax.axis_index("head")
    seq = lax.axis_index("seq")
    rows, shard = tok_ref.shape
    lanes = span_ref.shape[0]
    per_owner = down_hbm.shape[0]
    rank = down_hbm.shape[1]
    slice_rows = rows // lanes
    piece = rows // PIECES
    half = n // 2
    here = position_of(me, n)
    right = head_at(lax.rem(here + 1, n), n)
    left = head_at(lax.rem(here + n - 1, n), n)
    toward = (right, left)

    loads = [
        pltpu.make_async_copy(w_hbm.at[c], wbuf.at[:, pl.ds(c * P_SIZE, P_SIZE)], w_sem.at[c])
        for c in range(4)
    ]
    loads.append(pltpu.make_async_copy(down_hbm, dturn, w_sem.at[4]))

    barrier = pltpu.get_barrier_semaphore()

    def greet_head(d, carry):
        pl.semaphore_signal(
            barrier, inc=1, device_id={"head": lax.rem(me + d, n)}, device_id_type=MESH
        )
        return carry

    def greet_seq(d, carry):
        pl.semaphore_signal(
            barrier, inc=1, device_id={"seq": lax.rem(seq + d, n_seq)}, device_id_type=MESH
        )
        return carry

    lax.fori_loop(1, n, greet_head, 0)
    lax.fori_loop(1, n_seq, greet_seq, 0)
    for load in loads:
        load.start()
    pl.semaphore_wait(barrier, n - 1 + n_seq - 1)

    def hop(direction, step, p, own=False):
        span = pl.ds(p * piece, piece)
        source = tok_ref.at[span] if own else slots.at[direction, step - 2, span]
        return pltpu.make_async_remote_copy(
            src_ref=source,
            dst_ref=slots.at[direction, step - 1, span],
            send_sem=ring_send.at[direction, step - 1, p],
            recv_sem=ring_recv.at[direction, step - 1, p],
            device_id={"head": toward[direction]},
            device_id_type=MESH,
        )

    def long_way(direction, p):
        return p % 2 == direction

    for k in range(PIECES):
        for direction in range(2):
            hop(direction, 1, (k + direction) % PIECES, own=True).start()

    places = [owner_ref[prompt_ref[span_ref[j, seq]]] for j in range(lanes)]
    owned = [
        [jnp.where(places[j] == me * per_owner + s, 1.0, 0.0).astype(jnp.float32) for s in range(per_owner)]
        for j in range(lanes)
    ]

    for j in range(lanes):
        mine = sum(owned[j][s] * up_ref[s].astype(jnp.float32) for s in range(per_owner)).astype(jnp.bfloat16)
        for i in range(n):
            up_send[i, pl.ds(j * rank, rank), :] = mine[:, i * P_SIZE : (i + 1) * P_SIZE]

    def up_copy(d):
        peer = lax.rem(me + d, n)
        return pltpu.make_async_remote_copy(
            src_ref=up_send.at[peer],
            dst_ref=up_recv.at[d],
            send_sem=up_ssem.at[d],
            recv_sem=up_rsem.at[d],
            device_id={"head": peer},
            device_id_type=MESH,
        )

    def up_start(d, carry):
        up_copy(d).start()
        return carry

    lax.fori_loop(1, n, up_start, 0)
    up_recv[0] = up_send[me]

    for load in loads:
        load.wait()

    strip = wbuf.shape[0] // 12

    def turn_strip(i, carry):
        deep = pl.ds(pl.multiple_of(i * strip, strip), strip)
        for s in range(per_owner):
            dbuf[s, deep, :] = dturn[s, :, deep].T
        return carry

    lax.fori_loop(0, 12, turn_strip, 0)

    def multiply(x, span, origin, first=False):
        deep = pl.ds(pl.multiple_of(origin * shard, 64), shard)
        gained = dot(x, wbuf[deep, :])
        lows = [dot(x, dbuf[s, deep, :]) for s in range(per_owner)]
        if first:
            acc[span, :] = gained
            for s in range(per_owner):
                lacc[s, span, :] = lows[s]
        else:
            acc[span, :] += gained
            for s in range(per_owner):
                lacc[s, span, :] += lows[s]

    def own_piece(p, carry):
        span = pl.ds(pl.multiple_of(p * piece, piece), piece)
        multiply(tok_ref[span, :], span, me, first=True)
        return carry

    lax.fori_loop(0, PIECES, own_piece, 0)

    def arrive(step, forward, present):
        order = [((k + d) % PIECES, d) for k in range(PIECES) for d in range(2)]
        order = [(p, d) for p, d in order if present(d, p)]
        for p, d in order:
            hop(d, step, p).wait_recv() if not isinstance(step, int) or step > 1 else hop(d, 1, p, own=True).wait_recv()
            if forward(d, p):
                hop(d, step + 1, p).start()
            sign = n - step if d == 0 else step
            origin = head_at(lax.rem(here + sign, n), n)
            span = pl.ds(p * piece, piece)
            multiply(slots[d, step - 1, span, :], span, origin)

    everything = lambda d, p: True
    nothing = lambda d, p: False
    if half >= 2:
        arrive(1, everything if half > 2 else long_way, everything)
    if half > 3:

        def middle(step, carry):
            arrive(step, everything, everything)
            return carry

        lax.fori_loop(2, half - 1, middle, 0)
    if half > 2:
        arrive(half - 1, long_way, everything)
    arrive(half, nothing, long_way)

    width = lanes * rank
    for j in range(lanes):
        span = pl.ds(j * slice_rows, slice_rows)
        mine = sum(owned[j][s] * lacc[s, span, :] for s in range(per_owner)).astype(jnp.bfloat16)
        low_send[:, pl.ds(j * rank, rank)] = mine
    block = slice_rows // n

    def rs_copy(d):
        peer = lax.rem(me + d, n)
        return pltpu.make_async_remote_copy(
            src_ref=low_send.at[pl.ds(pl.multiple_of(peer * block, block), block)],
            dst_ref=low_recv.at[d],
            send_sem=rs_ssem.at[d],
            recv_sem=rs_rsem.at[d],
            device_id={"head": peer},
            device_id_type=MESH,
        )

    def ag_copy(d):
        peer = lax.rem(me + d, n)
        return pltpu.make_async_remote_copy(
            src_ref=low_recv.at[0],
            dst_ref=low_full.at[me],
            send_sem=ag_ssem.at[d],
            recv_sem=ag_rsem.at[d],
            device_id={"head": peer},
            device_id_type=MESH,
        )

    def ag_arrival(d):
        peer = lax.rem(me + n - d, n)
        return pltpu.make_async_remote_copy(
            src_ref=low_recv.at[0],
            dst_ref=low_full.at[peer],
            send_sem=ag_ssem.at[d],
            recv_sem=ag_rsem.at[d],
            device_id={"head": peer},
            device_id_type=MESH,
        )

    def each(count, act):
        def turn(d, carry):
            act(d)
            return carry

        lax.fori_loop(1, count, turn, 0)

    each(n, lambda d: rs_copy(d).start())
    each(n, lambda d: up_copy(d).wait_recv())
    up = jnp.sum(up_recv[...].astype(jnp.float32), axis=0).astype(jnp.bfloat16)
    total = low_send[pl.ds(pl.multiple_of(me * block, block), block), :].astype(jnp.float32)
    each(n, lambda d: rs_copy(d).wait_recv())
    for d in range(1, n):
        total = total + low_recv[d].astype(jnp.float32)
    low_recv[0] = total.astype(jnp.bfloat16)
    each(n, lambda d: ag_copy(d).start())
    low_full[me] = total.astype(jnp.bfloat16)

    slot_ids = lax.broadcasted_iota(jnp.int32, (slice_rows, 1), 0)
    causal = lax.broadcasted_iota(jnp.int32, (slice_rows, slice_rows), 0) >= lax.broadcasted_iota(
        jnp.int32, (slice_rows, slice_rows), 1
    )
    triangle = jnp.where(causal, 1.0, 0.0).astype(jnp.float32)
    columns = lax.broadcasted_iota(jnp.int32, (1, width), 1)
    each(n, lambda d: ag_arrival(d).wait_recv())
    low = low_full[...].reshape(slice_rows, width).astype(jnp.float32)

    kept = []
    for j in range(lanes):
        span = pl.ds(j * slice_rows, slice_rows)
        own = (columns >= j * rank) & (columns < (j + 1) * rank)
        gate = acc[span, pl.ds(3 * P_SIZE, P_SIZE)] + dot(jnp.where(own, low, 0.0).astype(jnp.bfloat16), up)
        live = jnp.where(slot_ids < len_ref[j, seq], 1.0, 0.0).astype(jnp.float32)
        step_log = -(live * rate_ref[...] * (2.0 * jax.nn.sigmoid(gate)))
        cumul = dot(triangle, step_log, HIGHEST)
        query = acc[span, pl.ds(0, P_SIZE)].astype(jnp.bfloat16).astype(jnp.float32)
        key = acc[span, pl.ds(P_SIZE, P_SIZE)].astype(jnp.bfloat16).astype(jnp.float32) * (
            live * P_SIZE ** (-0.5)
        )
        value = acc[span, pl.ds(2 * P_SIZE, P_SIZE)].astype(jnp.bfloat16).astype(jnp.float32)
        last = cumul[slice_rows - 1 :, :]
        carried = lax.dot_general(
            key * jnp.exp(last - cumul),
            value,
            (((0,), (0,)), ((), ())),
            precision=HIGHEST,
            preferred_element_type=jnp.float32,
        )
        st_send[j, pl.ds(0, P_SIZE), :] = carried
        st_send[j, pl.ds(P_SIZE, 8), :] = jnp.broadcast_to(jnp.exp(last), (8, P_SIZE))
        kept.append((live, query * jnp.exp(cumul), key * jnp.exp(-cumul), value))

    def st_copy(d):
        return pltpu.make_async_remote_copy(
            src_ref=st_send,
            dst_ref=st_recv.at[seq],
            send_sem=st_ssem.at[d],
            recv_sem=st_rsem.at[d],
            device_id={"seq": lax.rem(seq + d, n_seq)},
            device_id_type=MESH,
        )

    def st_arrival(d):
        peer = lax.rem(seq + n_seq - d, n_seq)
        return pltpu.make_async_remote_copy(
            src_ref=st_send,
            dst_ref=st_recv.at[peer],
            send_sem=st_ssem.at[d],
            recv_sem=st_rsem.at[d],
            device_id={"seq": peer},
            device_id_type=MESH,
        )

    each(n_seq, lambda d: st_copy(d).start())
    st_recv[seq] = st_send[...]

    inners = []
    for j in range(lanes):
        live, query_decay, key_decay, value = kept[j]
        scores = lax.dot_general(
            query_decay,
            key_decay,
            (((1,), (1,)), ((), ())),
            precision=HIGHEST,
            preferred_element_type=jnp.float32,
        )
        inners.append(dot(jnp.where(causal, scores, 0.0), value, HIGHEST))

    each(n_seq, lambda d: st_arrival(d).wait_recv())
    for j in range(lanes):
        live, query_decay, _, _ = kept[j]
        span = pl.ds(j * slice_rows, slice_rows)
        ended = jnp.zeros((P_SIZE, P_SIZE), jnp.float32)
        start = ended
        final = ended
        for k in range(n_seq):
            if k:
                same = jnp.where(span_ref[j, k] == span_ref[j, k - 1], 1.0, 0.0).astype(jnp.float32)
                begun = same * ended
            else:
                begun = ended
            decay = jnp.broadcast_to(st_recv[k, j, pl.ds(P_SIZE, 1), :], (P_SIZE, P_SIZE)).T
            ended = decay * begun + st_recv[k, j, pl.ds(0, P_SIZE), :]
            at = jnp.where(seq == k, 1.0, 0.0).astype(jnp.float32)
            start = start + at * begun
            final = final + at * ended
        inner = inners[j] + dot(query_decay, start, HIGHEST)
        scale = lax.rsqrt(jnp.maximum(jnp.mean(inner * inner, axis=-1, keepdims=True), NORM_FLOOR))
        out_ref[span, :] = (inner * scale * gain_ref[...] * live).astype(jnp.bfloat16)
        state_ref[0, j] = final

    each(n, lambda d: up_copy(d).wait_send())
    each(n, lambda d: rs_copy(d).wait_send())
    each(n, lambda d: ag_copy(d).wait_send())
    each(n_seq, lambda d: st_copy(d).wait_send())
    for p in range(PIECES):
        for direction in range(2):
            hop(direction, 1, p, own=True).wait_send()
    for direction in range(2):
        for p in range(PIECES):
            reach = half if long_way(direction, p) else half - 1

            def drained(step, carry):
                hop(direction, step, p).wait_send()
                return carry

            lax.fori_loop(2, reach + 1, drained, 0)


def solution(mesh):
    n, n_seq = mesh.shape["head"], mesh.shape["seq"]

    def body(
        tokens,
        proj_weight,
        decay_rate,
        norm_gain,
        pool_down,
        pool_up,
        span_id,
        prompt_adapter,
        owner_pos,
        slice_len,
    ):
        rows, shard = tokens.shape
        model = proj_weight.shape[1]
        lanes = span_id.shape[1]
        per_owner, _, rank = pool_down.shape
        slice_rows = rows // lanes
        width = lanes * rank
        smem = pl.BlockSpec(memory_space=pltpu.SMEM)
        vmem = pl.BlockSpec(memory_space=pltpu.VMEM)
        hbm = pl.BlockSpec(memory_space=pl.ANY)
        dma = pltpu.SemaphoreType.DMA
        return pl.pallas_call(
            functools.partial(kernel, n, n_seq),
            out_shape=(
                jax.ShapeDtypeStruct((rows, P_SIZE), jnp.bfloat16),
                jax.ShapeDtypeStruct((1, lanes, P_SIZE, P_SIZE), jnp.float32),
            ),
            in_specs=[smem, smem, smem, smem, vmem, hbm, hbm, vmem, vmem, vmem],
            out_specs=(vmem, vmem),
            scratch_shapes=[
                pltpu.VMEM((2, n // 2, rows, shard), jnp.bfloat16),
                pltpu.VMEM((model, 4 * P_SIZE), jnp.bfloat16),
                pltpu.VMEM((per_owner, model, rank), jnp.bfloat16),
                pltpu.VMEM((per_owner, rank, model), jnp.bfloat16),
                pltpu.VMEM((rows, 4 * P_SIZE), jnp.float32),
                pltpu.VMEM((per_owner, rows, rank), jnp.float32),
                pltpu.VMEM((n, width, P_SIZE), jnp.bfloat16),
                pltpu.VMEM((n, width, P_SIZE), jnp.bfloat16),
                pltpu.VMEM((slice_rows, width), jnp.bfloat16),
                pltpu.VMEM((n, slice_rows // n, width), jnp.bfloat16),
                pltpu.VMEM((n, slice_rows // n, width), jnp.bfloat16),
                pltpu.VMEM((lanes, P_SIZE + 8, P_SIZE), jnp.float32),
                pltpu.VMEM((n_seq, lanes, P_SIZE + 8, P_SIZE), jnp.float32),
                dma((5,)),
                dma((2, n // 2, PIECES)),
                dma((2, n // 2, PIECES)),
                dma((n,)),
                dma((n,)),
                dma((n,)),
                dma((n,)),
                dma((n,)),
                dma((n,)),
                dma((n_seq,)),
                dma((n_seq,)),
            ],
            compiler_params=pltpu.CompilerParams(
                collective_id=0, has_side_effects=True, vmem_limit_bytes=58 * 1024 * 1024
            ),
        )(
            span_id.T,
            prompt_adapter,
            owner_pos,
            slice_len.T,
            tokens,
            proj_weight,
            jnp.swapaxes(pool_down, 1, 2),
            pool_up,
            decay_rate.reshape(1, -1),
            norm_gain.reshape(1, -1),
        )

    in_specs = (
        P("seq", "head"),
        P(None, None, "head"),
        P("head"),
        P("head"),
        P("head", None, None),
        P("head", None, None),
        P(),
        P(),
        P(),
        P(),
    )
    out_specs = (P("seq", "head"), P("seq", None, "head", None))
    return jax.shard_map(body, mesh=mesh, in_specs=in_specs, out_specs=out_specs, check_vma=False)
```
